512 devices in a mesh: req: 64 (over x, z, core), pre: 8 (over y).
Axes of the slice: x: 4, y: 8, z: 8, core: 2. Of those that a mesh axis runs over, the one named last changes fastest.
Arguments:
- queries_raw: bfloat16 [16384, 3072], P('req', 'pre'), may hold values from -60 to 60
- keys_raw: bfloat16 [16384, 3072], P('req', 'pre'), may hold values from -60 to 60
- values: bfloat16 [16384, 3072], P('req', 'pre'), may hold values from -6 to 6
- query_gain: float32 [3072], P('pre'), may hold values from 1 to 3
- key_gain: float32 [3072], P('pre'), may hold values from 1 to 3
- prefix_keys: bfloat16 [8192, 3072], P('req', 'pre'), may hold values from -16 to 16
- prefix_values: bfloat16 [8192, 3072], P('req', 'pre'), may hold values from -6 to 6
- segment_ids: int32 [64, 256], P('req'), may hold values from 0 to 7, never falling along the last dimension, each value on 1 to 64 neighbouring positions
- live_rows: int32 [64], P('req'), may hold values from 64 to 256, as said below
Outputs:
- attended: bfloat16 [16384, 3072], P('req', 'pre')
- suffix_keys: bfloat16 [16384, 3072], P('req', 'pre')
The draws below stay inside these ranges and needn't reach their ends.
Inputs may be any that keep to these rules, and one draw needn't show every extreme that they name: `live_rows`: every group has at least 64 live rows; some group has all 256 rows live in every draw. `segment_ids`: in each group the request numbers never fall along the rows; a request has at most 64 rows.
All inputs are finite; a program needn't handle non-finite values.
Results may differ from the reference program's by a relative error of at most 0.011.
Values may be sent and summed in bfloat16 or wider, within the bound.
A program may use at most 128 MiB of HBM per device.

```python
import math
import jax
import jax.numpy as jnp
import numpy as np
from jax import lax

HEADS = 24
HD = 128
ROWS = 256
PRE_DEV = 128
REQS = 8
GROUPS = 64
PREFIX = 8192


def column_scale(column_key, full_width):
    ramp = jnp.exp(math.log(3.0) * jnp.arange(full_width, dtype=jnp.float32) / max(full_width - 1, 1))
    return ramp * jnp.exp(jax.random.uniform(column_key, (full_width,), jnp.float32, 0.0, math.log(10.0)))


def projected_rows(base_key, salt):
    row_total = GROUPS * ROWS
    full_width = HEADS * HD
    own_key = jax.random.fold_in(base_key, salt)
    value_key, row_key, column_key = jax.random.split(own_key, 3)
    row_scale = jnp.exp(jax.random.uniform(row_key, (row_total, 1), jnp.float32, 0.0, math.log(10.0)))
    columns = column_scale(column_key, full_width)
    noise = jax.random.normal(value_key, (row_total, full_width), jnp.float32)
    dense = jnp.clip(noise * row_scale * columns[None, :] * 0.1, -60.0, 60.0)
    return dense


def draw_queries_raw(key, part):
    return projected_rows(key, 1).astype(jnp.bfloat16)


def draw_keys_raw(key, part):
    return projected_rows(key, 2).astype(jnp.bfloat16)


def draw_prefix_keys(key, part):
    full_width = HEADS * HD
    own_key = jax.random.fold_in(key, 3)
    value_key, column_key = jax.random.split(own_key, 2)
    columns = jnp.exp(jax.random.uniform(column_key, (full_width,), jnp.float32, 0.0, math.log(2.0)))
    dense = 1.5 * jax.random.normal(value_key, (PREFIX, full_width), jnp.float32) * columns[None, :]
    return jnp.clip(dense, -16.0, 16.0).astype(jnp.bfloat16)


def draw_live_rows(key, part):
    own_key = jax.random.fold_in(key, 5)
    length_key, full_key = jax.random.split(own_key, 2)
    lengths = jax.random.randint(length_key, (GROUPS,), ROWS // 4, ROWS + 1)
    full_group = jax.random.randint(full_key, (), 0, GROUPS)
    return jnp.where(jnp.arange(GROUPS) == full_group, ROWS, lengths).astype(jnp.int32)


def steps_of(key, shape, cuts, smallest, largest):
    loudness, own = 1.0, jax.random.fold_in(key, 6)
    for dim, parts in cuts:
        heights = jnp.exp(jax.random.uniform(jax.random.fold_in(own, dim), (parts,), jnp.float32, smallest / len(cuts), largest / len(cuts)))
        loudness = loudness * jnp.repeat(heights, shape[dim] // parts).reshape([-1 if axis == dim else 1 for axis in range(len(shape))])
    return loudness


def length_profile(number_of, total, most, slope):
    weights = [(1 << 20) // math.isqrt(rank ** slope) + 1 for rank in range(2, number_of + 1)]
    spare, holding = total - most - (number_of - 1), [1] * (number_of - 1)
    while spare > 0:
        movable = [i for i in range(number_of - 1) if holding[i] < most]
        mass, budget = sum([weights[i] for i in movable]), spare
        for i in movable:
            addition = min(most - holding[i], max(1, budget * weights[i] // mass), spare)
            holding[i] = holding[i] + addition
            spare = spare - addition
    return np.array([most] + holding)


def uneven_parts(key, number_of, total, bound, slope):
    if number_of == 2:
        one = jax.random.randint(key, (), max(1, total - bound), min(bound, total - 1) + 1)
        return jnp.stack([one, total - one])
    sizes = jnp.asarray(length_profile(number_of, total, bound, slope), jnp.int32)
    twos = (number_of - 1) // 2
    donor, sink = sizes[1:1 + 2 * twos:2], sizes[2:2 + 2 * twos:2]
    slack = jnp.minimum(donor - 1, bound - sink)
    passed = jax.random.randint(jax.random.fold_in(key, 1), (twos,), 0, 1 << 20) % (slack + 1)
    sizes = sizes.at[1:1 + 2 * twos:2].set(donor - passed).at[2:2 + 2 * twos:2].set(sink + passed)
    return sizes[jax.random.permutation(jax.random.fold_in(key, 2), number_of)]


def scatter_about(rng, extent, spread, most, cuts=(), kind=jnp.bfloat16):
    loudness = steps_of(rng, extent, cuts, -0.22, 0.18) if cuts else 1.0
    result = jax.random.normal(rng, extent, jnp.float32) * spread * loudness
    return jnp.minimum(jnp.maximum(result, -most), most).astype(kind)


def setup_inputs(seed: int = 0) -> dict:
    arg_keys = jax.random.split(jax.random.key(seed), 10)
    queries_raw = draw_queries_raw(jax.random.fold_in(arg_keys[9], 71), 0)
    keys_raw = draw_keys_raw(jax.random.fold_in(arg_keys[9], 71), 0)
    values = scatter_about(arg_keys[2], (GROUPS * ROWS, HEADS * HD), 1.0, 6.0, ((0, 64), (1, 8)))
    query_gain = jnp.clip(jnp.exp(math.log(3.0) - 1.0986123 * jax.random.uniform(arg_keys[3], (HEADS * HD,), jnp.float32) ** steps_of(arg_keys[3], (HEADS * HD,), ((0, 8),), -0.2, 0.2)), 1.0, 3.0)
    key_gain = jnp.clip(jnp.exp(math.log(3.0) - 1.0986123 * jax.random.uniform(arg_keys[4], (HEADS * HD,), jnp.float32) ** steps_of(arg_keys[4], (HEADS * HD,), ((0, 8),), -0.2, 0.2)), 1.0, 3.0)
    prefix_keys = draw_prefix_keys(jax.random.fold_in(arg_keys[9], 71), 0)
    prefix_values = scatter_about(arg_keys[6], (PREFIX, HEADS * HD), 1.0, 6.0, ((0, 64), (1, 8)))
    segment_ids = jax.vmap(lambda own: jnp.searchsorted(jnp.cumsum(uneven_parts(own, REQS, ROWS, ROWS // 4, 2)), jnp.arange(ROWS), side="right"))(jax.random.split(arg_keys[7], GROUPS)).reshape((GROUPS, ROWS)).astype(jnp.int32)
    live_rows = draw_live_rows(jax.random.fold_in(arg_keys[9], 71), 0)
    return {"queries_raw": queries_raw, "keys_raw": keys_raw, "values": values, "query_gain": query_gain, "key_gain": key_gain, "prefix_keys": prefix_keys, "prefix_values": prefix_values, "segment_ids": segment_ids, "live_rows": live_rows}


epsilon = 1e-06
rope_base = 500000.0
floor_value = -1e+30

def rotate(vectors, position):
    half_dim = vectors.shape[-1] // 2
    inverse = jnp.exp(-math.log(rope_base) * 2.0 * jnp.arange(half_dim, dtype=jnp.float32) / vectors.shape[-1])
    angles = position.astype(jnp.float32)[:, None] * inverse[None, :]
    cosine = jnp.cos(angles)[:, None, :]
    sine_part = jnp.sin(angles)[:, None, :]
    first_half = vectors[..., :half_dim]
    second_half = vectors[..., half_dim:]
    return jnp.concatenate([first_half * cosine - second_half * sine_part, second_half * cosine + first_half * sine_part], axis=-1)

def positions(segment, prefix_len):
    row_index = jnp.arange(segment.shape[0], dtype=jnp.int32)
    first_row = lax.optimization_barrier(jnp.sum((segment[None, :] < segment[:, None]).astype(jnp.int32), axis=1))
    return prefix_len + row_index - first_row

def reference(queries_raw, keys_raw, values, query_gain, key_gain, prefix_keys, prefix_values, segment_ids, live_rows):
    group_count = live_rows.shape[0]
    full_width = HEADS * HD
    query_f = queries_raw.astype(jnp.float32)
    key_f = keys_raw.astype(jnp.float32)
    normed_q = query_f * lax.rsqrt(lax.optimization_barrier(jnp.mean(query_f * query_f, axis=1, keepdims=True)) + epsilon) * query_gain[None, :]
    normed_k = key_f * lax.rsqrt(lax.optimization_barrier(jnp.mean(key_f * key_f, axis=1, keepdims=True)) + epsilon) * key_gain[None, :]
    prefix_len = prefix_keys.shape[0]
    block_count = prefix_len // PRE_DEV
    prefix_k = prefix_keys.astype(jnp.float32).reshape(block_count, PRE_DEV, HEADS, HD)
    prefix_v = prefix_values.astype(jnp.float32).reshape(block_count, PRE_DEV, HEADS, HD)
    scaling = 1.0 / math.sqrt(HD)

    def one_group(item):
        group_q, group_k, group_v, segment, live_count = item
        position = positions(segment, prefix_len)
        queries_bf = rotate(group_q.reshape(ROWS, HEADS, HD), position).astype(jnp.bfloat16)
        rotated_k = rotate(group_k.reshape(ROWS, HEADS, HD), position).astype(jnp.bfloat16)
        row_index = jnp.arange(ROWS, dtype=jnp.int32)
        alive = row_index < live_count
        suffix_cache = jnp.where(alive[:, None, None], rotated_k, jnp.zeros_like(rotated_k))
        query_w = lax.optimization_barrier(queries_bf).astype(jnp.float32)
        scores = jnp.einsum('qhd,bkhd->bhqk', query_w, prefix_k) * scaling
        block_max = lax.optimization_barrier(jnp.max(scores, axis=-1))
        weights = jnp.exp(scores - block_max[..., None])
        block_sum = lax.optimization_barrier(jnp.sum(weights, axis=-1))
        rounded = lax.optimization_barrier(weights.astype(jnp.bfloat16)).astype(jnp.float32)
        block_out = jnp.einsum('bhqk,bkhd->bhqd', rounded, prefix_v) / block_sum[..., None]
        block_out = lax.optimization_barrier(block_out.astype(jnp.bfloat16)).astype(jnp.float32)
        cache_w = lax.optimization_barrier(suffix_cache).astype(jnp.float32)
        own_scores = jnp.einsum('qhd,khd->hqk', query_w, cache_w) * scaling
        allowed = (segment[None, :] == segment[:, None]) & (row_index[None, :] <= row_index[:, None]) & alive[None, :]
        own_max = lax.optimization_barrier(jnp.max(jnp.where(allowed[None], own_scores, floor_value), axis=-1))
        own_weights = jnp.exp(jnp.where(allowed[None], own_scores - own_max[..., None], floor_value))
        own_sum = lax.optimization_barrier(jnp.sum(own_weights, axis=-1))
        own_rounded = lax.optimization_barrier(own_weights.astype(jnp.bfloat16)).astype(jnp.float32)
        own_values = group_v.reshape(ROWS, HEADS, HD).astype(jnp.float32)
        own_out = jnp.einsum('hqk,khd->hqd', own_rounded, own_values) / jnp.maximum(own_sum, 1.0)[..., None]
        own_out = lax.optimization_barrier(own_out.astype(jnp.bfloat16)).astype(jnp.float32)
        best = jnp.maximum(lax.optimization_barrier(jnp.max(block_max, axis=0)), own_max)
        block_weight = block_sum * jnp.exp(block_max - best[None])
        own_weight = own_sum * jnp.exp(own_max - best)
        numerator = lax.optimization_barrier(jnp.sum(block_weight[..., None] * block_out, axis=0)) + own_weight[..., None] * own_out
        denominator = lax.optimization_barrier(jnp.sum(block_weight, axis=0)) + own_weight
        merged = jnp.transpose(numerator / denominator[..., None], (1, 0, 2)).reshape(ROWS, full_width)
        attended = jnp.where(alive[:, None], merged, 0.0).astype(jnp.bfloat16)
        return (attended, suffix_cache.reshape(ROWS, full_width))
    attended, caches = lax.map(one_group, (normed_q.reshape(group_count, ROWS, full_width), normed_k.reshape(group_count, ROWS, full_width), values.reshape(group_count, ROWS, full_width), segment_ids, live_rows))
    return (attended.reshape(group_count * ROWS, full_width), caches.reshape(group_count * ROWS, full_width))
```

```python
import math

import jax
import jax.numpy as jnp
from jax import lax
from jax.experimental import pallas as pl
from jax.experimental.pallas import tpu as pltpu
from jax.sharding import PartitionSpec as P

HD = 128
KV_BLOCK = 2048


epsilon = 1e-06
rope_base = 500000.0
floor_value = -1e30


def rotate(vectors, position):
    half_dim = vectors.shape[-1] // 2
    inverse = jnp.exp(
        -math.log(rope_base) * 2.0 * jnp.arange(half_dim, dtype=jnp.float32) / vectors.shape[-1]
    )
    angles = position.astype(jnp.float32)[:, None] * inverse[None, :]
    cosine = jnp.cos(angles)[:, None, :]
    sine_part = jnp.sin(angles)[:, None, :]
    first_half = vectors[..., :half_dim]
    second_half = vectors[..., half_dim:]
    return jnp.concatenate(
        [
            first_half * cosine - second_half * sine_part,
            second_half * cosine + first_half * sine_part,
        ],
        axis=-1,
    )


def positions(segment, prefix_len):
    row_index = jnp.arange(segment.shape[0], dtype=jnp.int32)
    first_row = jnp.sum((segment[None, :] < segment[:, None]).astype(jnp.int32), axis=1)
    return prefix_len + row_index - first_row


def flash_kernel(
    q_ref, k_ref, v_ref, oo_ref, om_ref, os_ref, alive_ref, out_ref, m_sc, l_sc, acc_sc, *, scaling
):
    j = pl.program_id(1)

    @pl.when(j == 0)
    def _():
        m_sc[...] = jnp.full(m_sc.shape, floor_value, jnp.float32)
        l_sc[...] = jnp.zeros(l_sc.shape, jnp.float32)
        acc_sc[...] = jnp.zeros(acc_sc.shape, jnp.float32)

    s = (
        lax.dot_general(
            q_ref[...],
            k_ref[...],
            (((1,), (1,)), ((), ())),
            preferred_element_type=jnp.float32,
        )
        * scaling
    )
    m_prev = m_sc[...]
    m_new = jnp.maximum(m_prev, jnp.max(s, axis=1, keepdims=True))
    alpha = jnp.exp(m_prev - m_new)
    p = jnp.exp(s - m_new)
    l_sc[...] = alpha * l_sc[...] + jnp.sum(p, axis=1, keepdims=True)
    acc_sc[...] = alpha * acc_sc[...] + jnp.dot(
        p.astype(jnp.bfloat16), v_ref[...], preferred_element_type=jnp.float32
    )
    m_sc[...] = m_new

    @pl.when(j == pl.num_programs(1) - 1)
    def _():
        m = m_sc[...]
        own_max = om_ref[...]
        best = jnp.maximum(m, own_max)
        prefix_weight = jnp.exp(m - best)
        own_weight = os_ref[...] * jnp.exp(own_max - best)
        numerator = acc_sc[...] * prefix_weight + own_weight * oo_ref[...].astype(jnp.float32)
        denominator = l_sc[...] * prefix_weight + own_weight
        merged = numerator / denominator
        out_ref[...] = jnp.where(alive_ref[...] > 0.0, merged, 0.0).astype(out_ref.dtype)


def prefix_attention(queries2d, kv_rows, own_out2d, own_max, own_sum, alive_f, head_count, scaling):
    row_count = queries2d.shape[0]
    total = kv_rows.shape[0]
    block = min(KV_BLOCK, total)
    steps = total // block
    kernel = lambda *refs: flash_kernel(*refs, scaling=scaling)
    return pl.pallas_call(
        kernel,
        grid=(head_count, steps),
        in_specs=[
            pl.BlockSpec((row_count, HD), lambda h, j: (0, h)),
            pl.BlockSpec((block, HD), lambda h, j: (j, h)),
            pl.BlockSpec((block, HD), lambda h, j: (j, head_count + h)),
            pl.BlockSpec((row_count, HD), lambda h, j: (0, h)),
            pl.BlockSpec((None, row_count, 1), lambda h, j: (h, 0, 0)),
            pl.BlockSpec((None, row_count, 1), lambda h, j: (h, 0, 0)),
            pl.BlockSpec((row_count, 1), lambda h, j: (0, 0)),
        ],
        out_specs=pl.BlockSpec((row_count, HD), lambda h, j: (0, h)),
        out_shape=jax.ShapeDtypeStruct((row_count, head_count * HD), jnp.bfloat16),
        scratch_shapes=[
            pltpu.VMEM((row_count, 1), jnp.float32),
            pltpu.VMEM((row_count, 1), jnp.float32),
            pltpu.VMEM((row_count, HD), jnp.float32),
        ],
        compiler_params=pltpu.CompilerParams(dimension_semantics=("arbitrary", "arbitrary")),
    )(queries2d, kv_rows, kv_rows, own_out2d, own_max, own_sum, alive_f)


def per_device(
    queries_raw,
    keys_raw,
    values,
    query_gain,
    key_gain,
    prefix_keys,
    prefix_values,
    segment_ids,
    live_rows,
):
    row_count, local_width = queries_raw.shape
    head_count = local_width // HD
    kv_block = jnp.concatenate([prefix_keys, prefix_values], axis=1)
    kv_rows = lax.all_gather(kv_block, "req", axis=0, tiled=True)
    query_f = queries_raw.astype(jnp.float32)
    key_f = keys_raw.astype(jnp.float32)
    square_q, square_k = lax.psum(
        (jnp.sum(query_f * query_f, axis=1), jnp.sum(key_f * key_f, axis=1)), "pre"
    )
    full_width = local_width * lax.axis_size("pre")
    normed_q = query_f * lax.rsqrt(square_q / full_width + epsilon)[:, None] * query_gain[None, :]
    normed_k = key_f * lax.rsqrt(square_k / full_width + epsilon)[:, None] * key_gain[None, :]
    shard_rows = prefix_keys.shape[0]
    prefix_len = shard_rows * lax.axis_size("req")
    segment = segment_ids[0]
    live_count = live_rows[0]
    position = positions(segment, prefix_len)
    queries_bf = rotate(normed_q.reshape(row_count, head_count, HD), position).astype(jnp.bfloat16)
    rotated_k = rotate(normed_k.reshape(row_count, head_count, HD), position).astype(jnp.bfloat16)
    row_index = jnp.arange(row_count, dtype=jnp.int32)
    alive = row_index < live_count
    suffix_cache = jnp.where(alive[:, None, None], rotated_k, jnp.zeros_like(rotated_k))
    values_grid = values.reshape(row_count, head_count, HD)
    scaling = 1.0 / math.sqrt(HD)
    scores = (
        jnp.einsum("qhd,khd->hqk", queries_bf, suffix_cache, preferred_element_type=jnp.float32)
        * scaling
    )
    allowed = (
        (segment[None, :] == segment[:, None])
        & (row_index[None, :] <= row_index[:, None])
        & alive[None, :]
    )
    row_best = jnp.max(jnp.where(allowed[None], scores, floor_value), axis=-1)
    weights = jnp.exp(jnp.where(allowed[None], scores - row_best[..., None], floor_value))
    row_sum = jnp.sum(weights, axis=-1)
    summed = jnp.einsum(
        "hqk,khd->qhd",
        weights.astype(jnp.bfloat16),
        values_grid,
        preferred_element_type=jnp.float32,
    )
    suffix_out = (summed / jnp.maximum(row_sum, 1.0).T[:, :, None]).astype(jnp.bfloat16)
    attended = prefix_attention(
        queries_bf.reshape(row_count, local_width),
        kv_rows,
        suffix_out.reshape(row_count, local_width),
        row_best[:, :, None],
        row_sum[:, :, None],
        alive.astype(jnp.float32)[:, None],
        head_count,
        scaling,
    )
    return (attended, suffix_cache.reshape(row_count, local_width))


def solution(mesh):
    placed = (
        P("req", "pre"),
        P("req", "pre"),
        P("req", "pre"),
        P("pre"),
        P("pre"),
        P("req", "pre"),
        P("req", "pre"),
        P("req", None),
        P("req"),
    )
    return jax.shard_map(
        per_device,
        mesh=mesh,
        in_specs=placed,
        out_specs=(P("req", "pre"), P("req", "pre")),
        check_vma=False,
    )
```

```python
import math

import jax
import jax.numpy as jnp
from jax import lax
from jax.experimental import pallas as pl
from jax.experimental.pallas import tpu as pltpu
from jax.sharding import PartitionSpec as P

HD = 128
KV_BLOCK = 8192


epsilon = 1e-06
rope_base = 500000.0
floor_value = -1e30


def rotate(vectors, position):
    half_dim = vectors.shape[-1] // 2
    inverse = jnp.exp(
        -math.log(rope_base) * 2.0 * jnp.arange(half_dim, dtype=jnp.float32) / vectors.shape[-1]
    )
    angles = position.astype(jnp.float32)[:, None] * inverse[None, :]
    cosine = jnp.cos(angles)[:, None, :]
    sine_part = jnp.sin(angles)[:, None, :]
    first_half = vectors[..., :half_dim]
    second_half = vectors[..., half_dim:]
    return jnp.concatenate(
        [
            first_half * cosine - second_half * sine_part,
            second_half * cosine + first_half * sine_part,
        ],
        axis=-1,
    )


def positions(segment, prefix_len):
    row_index = jnp.arange(segment.shape[0], dtype=jnp.int32)
    first_row = jnp.sum((segment[None, :] < segment[:, None]).astype(jnp.int32), axis=1)
    return prefix_len + row_index - first_row


def flash_kernel(
    q_ref, k_ref, v_ref, oo_ref, om_ref, os_ref, alive_ref, out_ref, m_sc, l_sc, acc_sc, *, scaling
):
    j = pl.program_id(1)

    @pl.when(j == 0)
    def _():
        m_sc[...] = jnp.full(m_sc.shape, floor_value, jnp.float32)
        l_sc[...] = jnp.zeros(l_sc.shape, jnp.float32)
        acc_sc[...] = jnp.zeros(acc_sc.shape, jnp.float32)

    s = (
        lax.dot_general(
            q_ref[...],
            k_ref[...],
            (((1,), (1,)), ((), ())),
            preferred_element_type=jnp.float32,
        )
        * scaling
    )
    m_prev = m_sc[...]
    m_new = jnp.maximum(m_prev, jnp.max(s, axis=1, keepdims=True))
    alpha = jnp.exp(m_prev - m_new)
    p = jnp.exp(s - m_new)
    l_sc[...] = alpha * l_sc[...] + jnp.sum(p, axis=1, keepdims=True)
    acc_sc[...] = alpha * acc_sc[...] + jnp.dot(
        p.astype(jnp.bfloat16), v_ref[...], preferred_element_type=jnp.float32
    )
    m_sc[...] = m_new

    @pl.when(j == pl.num_programs(1) - 1)
    def _():
        m = m_sc[...]
        own_max = om_ref[...]
        best = jnp.maximum(m, own_max)
        prefix_weight = jnp.exp(m - best)
        own_weight = os_ref[...] * jnp.exp(own_max - best)
        numerator = acc_sc[...] * prefix_weight + own_weight * oo_ref[...].astype(jnp.float32)
        denominator = l_sc[...] * prefix_weight + own_weight
        merged = numerator / denominator
        out_ref[...] = jnp.where(alive_ref[...] > 0.0, merged, 0.0).astype(out_ref.dtype)


def prefix_attention(queries2d, kv_rows, own_out2d, own_max, own_sum, alive_f, head_count, scaling):
    row_count = queries2d.shape[0]
    total = kv_rows.shape[0]
    block = min(KV_BLOCK, total)
    steps = total // block
    kernel = lambda *refs: flash_kernel(*refs, scaling=scaling)
    return pl.pallas_call(
        kernel,
        grid=(head_count, steps),
        in_specs=[
            pl.BlockSpec((row_count, HD), lambda h, j: (0, h)),
            pl.BlockSpec((block, HD), lambda h, j: (j, h)),
            pl.BlockSpec((block, HD), lambda h, j: (j, head_count + h)),
            pl.BlockSpec((row_count, HD), lambda h, j: (0, h)),
            pl.BlockSpec((None, row_count, 1), lambda h, j: (h, 0, 0)),
            pl.BlockSpec((None, row_count, 1), lambda h, j: (h, 0, 0)),
            pl.BlockSpec((row_count, 1), lambda h, j: (0, 0)),
        ],
        out_specs=pl.BlockSpec((row_count, HD), lambda h, j: (0, h)),
        out_shape=jax.ShapeDtypeStruct((row_count, head_count * HD), jnp.bfloat16),
        scratch_shapes=[
            pltpu.VMEM((row_count, 1), jnp.float32),
            pltpu.VMEM((row_count, 1), jnp.float32),
            pltpu.VMEM((row_count, HD), jnp.float32),
        ],
        compiler_params=pltpu.CompilerParams(dimension_semantics=("arbitrary", "arbitrary")),
    )(queries2d, kv_rows, kv_rows, own_out2d, own_max, own_sum, alive_f)


def per_device(
    queries_raw,
    keys_raw,
    values,
    query_gain,
    key_gain,
    prefix_keys,
    prefix_values,
    segment_ids,
    live_rows,
):
    row_count, local_width = queries_raw.shape
    head_count = local_width // HD
    kv_block = jnp.concatenate([prefix_keys, prefix_values], axis=1)
    kv_rows = lax.all_gather(kv_block, "req", axis=0, tiled=True)
    query_f = queries_raw.astype(jnp.float32)
    key_f = keys_raw.astype(jnp.float32)
    square_q, square_k = lax.psum(
        (jnp.sum(query_f * query_f, axis=1), jnp.sum(key_f * key_f, axis=1)), "pre"
    )
    full_width = local_width * lax.axis_size("pre")
    normed_q = query_f * lax.rsqrt(square_q / full_width + epsilon)[:, None] * query_gain[None, :]
    normed_k = key_f * lax.rsqrt(square_k / full_width + epsilon)[:, None] * key_gain[None, :]
    shard_rows = prefix_keys.shape[0]
    prefix_len = shard_rows * lax.axis_size("req")
    segment = segment_ids[0]
    live_count = live_rows[0]
    position = positions(segment, prefix_len)
    queries_bf = rotate(normed_q.reshape(row_count, head_count, HD), position).astype(jnp.bfloat16)
    rotated_k = rotate(normed_k.reshape(row_count, head_count, HD), position).astype(jnp.bfloat16)
    row_index = jnp.arange(row_count, dtype=jnp.int32)
    alive = row_index < live_count
    suffix_cache = jnp.where(alive[:, None, None], rotated_k, jnp.zeros_like(rotated_k))
    values_grid = values.reshape(row_count, head_count, HD)
    scaling = 1.0 / math.sqrt(HD)
    scores = (
        jnp.einsum("qhd,khd->hqk", queries_bf, suffix_cache, preferred_element_type=jnp.float32)
        * scaling
    )
    allowed = (
        (segment[None, :] == segment[:, None])
        & (row_index[None, :] <= row_index[:, None])
        & alive[None, :]
    )
    row_best = jnp.max(jnp.where(allowed[None], scores, floor_value), axis=-1)
    weights = jnp.exp(jnp.where(allowed[None], scores - row_best[..., None], floor_value))
    row_sum = jnp.sum(weights, axis=-1)
    summed = jnp.einsum(
        "hqk,khd->qhd",
        weights.astype(jnp.bfloat16),
        values_grid,
        preferred_element_type=jnp.float32,
    )
    suffix_out = (summed / jnp.maximum(row_sum, 1.0).T[:, :, None]).astype(jnp.bfloat16)
    attended = prefix_attention(
        queries_bf.reshape(row_count, local_width),
        kv_rows,
        suffix_out.reshape(row_count, local_width),
        row_best[:, :, None],
        row_sum[:, :, None],
        alive.astype(jnp.float32)[:, None],
        head_count,
        scaling,
    )
    return (attended, suffix_cache.reshape(row_count, local_width))


def solution(mesh):
    placed = (
        P("req", "pre"),
        P("req", "pre"),
        P("req", "pre"),
        P("pre"),
        P("pre"),
        P("req", "pre"),
        P("req", "pre"),
        P("req", None),
        P("req"),
    )
    return jax.shard_map(
        per_device,
        mesh=mesh,
        in_specs=placed,
        out_specs=(P("req", "pre"), P("req", "pre")),
        check_vma=False,
    )
```

```python
import math

import jax
import jax.numpy as jnp
from jax import lax
from jax.experimental import pallas as pl
from jax.experimental.pallas import tpu as pltpu
from jax.sharding import PartitionSpec as P

HD = 128


epsilon = 1e-06
rope_base = 500000.0
floor_value = -1e30


def rotate(vectors, position):
    half_dim = vectors.shape[-1] // 2
    inverse = jnp.exp(
        -math.log(rope_base) * 2.0 * jnp.arange(half_dim, dtype=jnp.float32) / vectors.shape[-1]
    )
    angles = position.astype(jnp.float32)[:, None] * inverse[None, :]
    cosine = jnp.cos(angles)[:, None, :]
    sine_part = jnp.sin(angles)[:, None, :]
    first_half = vectors[..., :half_dim]
    second_half = vectors[..., half_dim:]
    return jnp.concatenate(
        [
            first_half * cosine - second_half * sine_part,
            second_half * cosine + first_half * sine_part,
        ],
        axis=-1,
    )


def positions(segment, prefix_len):
    row_index = jnp.arange(segment.shape[0], dtype=jnp.int32)
    first_row = jnp.sum((segment[None, :] < segment[:, None]).astype(jnp.int32), axis=1)
    return prefix_len + row_index - first_row


def flash_kernel(q_ref, k_ref, v_ref, oo_ref, om_ref, os_ref, alive_ref, out_ref):
    keys = k_ref[...].reshape(-1, HD)
    vals = v_ref[...].reshape(-1, HD)
    s = lax.dot_general(
        q_ref[...],
        keys,
        (((1,), (1,)), ((), ())),
        preferred_element_type=jnp.float32,
    )
    m = jnp.max(s, axis=1, keepdims=True)
    p = jnp.exp(s - m)
    prefix_sum = jnp.sum(p, axis=1, keepdims=True)
    prefix_acc = jnp.dot(p.astype(jnp.bfloat16), vals, preferred_element_type=jnp.float32)
    own_max = om_ref[...]
    best = jnp.maximum(m, own_max)
    prefix_weight = jnp.exp(m - best)
    own_weight = os_ref[...] * jnp.exp(own_max - best)
    numerator = prefix_acc * prefix_weight + own_weight * oo_ref[...].astype(jnp.float32)
    denominator = prefix_sum * prefix_weight + own_weight
    merged = numerator / denominator
    out_ref[...] = jnp.where(alive_ref[...] > 0.0, merged, 0.0).astype(out_ref.dtype)


def prefix_attention(scaled_q2d, kv_rows, own_out2d, own_max, own_sum, alive_f, head_count):
    row_count = scaled_q2d.shape[0]
    owners, _, shard_rows, _ = kv_rows.shape
    return pl.pallas_call(
        flash_kernel,
        grid=(head_count,),
        in_specs=[
            pl.BlockSpec((row_count, HD), lambda h: (0, h)),
            pl.BlockSpec((owners, None, shard_rows, HD), lambda h: (0, 0, 0, h)),
            pl.BlockSpec((owners, None, shard_rows, HD), lambda h: (0, 1, 0, h)),
            pl.BlockSpec((row_count, HD), lambda h: (0, h)),
            pl.BlockSpec((None, row_count, 1), lambda h: (h, 0, 0)),
            pl.BlockSpec((None, row_count, 1), lambda h: (h, 0, 0)),
            pl.BlockSpec((row_count, 1), lambda h: (0, 0)),
        ],
        out_specs=pl.BlockSpec((row_count, HD), lambda h: (0, h)),
        out_shape=jax.ShapeDtypeStruct((row_count, head_count * HD), jnp.bfloat16),
        compiler_params=pltpu.CompilerParams(dimension_semantics=("arbitrary",)),
    )(scaled_q2d, kv_rows, kv_rows, own_out2d, own_max, own_sum, alive_f)


def per_device(
    queries_raw,
    keys_raw,
    values,
    query_gain,
    key_gain,
    prefix_keys,
    prefix_values,
    segment_ids,
    live_rows,
):
    row_count, local_width = queries_raw.shape
    head_count = local_width // HD
    kv_block = jnp.stack([prefix_keys, prefix_values], axis=0)
    kv_rows = lax.all_gather(kv_block, "req", axis=0)
    query_f = queries_raw.astype(jnp.float32)
    key_f = keys_raw.astype(jnp.float32)
    square_q, square_k = lax.psum(
        (jnp.sum(query_f * query_f, axis=1), jnp.sum(key_f * key_f, axis=1)), "pre"
    )
    full_width = local_width * lax.axis_size("pre")
    normed_q = query_f * lax.rsqrt(square_q / full_width + epsilon)[:, None] * query_gain[None, :]
    normed_k = key_f * lax.rsqrt(square_k / full_width + epsilon)[:, None] * key_gain[None, :]
    shard_rows = prefix_keys.shape[0]
    prefix_len = shard_rows * lax.axis_size("req")
    segment = segment_ids[0]
    live_count = live_rows[0]
    position = positions(segment, prefix_len)
    rotated_q = rotate(normed_q.reshape(row_count, head_count, HD), position)
    queries_bf = rotated_q.astype(jnp.bfloat16)
    rotated_k = rotate(normed_k.reshape(row_count, head_count, HD), position).astype(jnp.bfloat16)
    row_index = jnp.arange(row_count, dtype=jnp.int32)
    alive = row_index < live_count
    suffix_cache = jnp.where(alive[:, None, None], rotated_k, jnp.zeros_like(rotated_k))
    values_grid = values.reshape(row_count, head_count, HD)
    scaling = 1.0 / math.sqrt(HD)
    scores = (
        jnp.einsum("qhd,khd->hqk", queries_bf, suffix_cache, preferred_element_type=jnp.float32)
        * scaling
    )
    allowed = (
        (segment[None, :] == segment[:, None])
        & (row_index[None, :] <= row_index[:, None])
        & alive[None, :]
    )
    row_best = jnp.max(jnp.where(allowed[None], scores, floor_value), axis=-1)
    weights = jnp.exp(jnp.where(allowed[None], scores - row_best[..., None], floor_value))
    row_sum = jnp.sum(weights, axis=-1)
    summed = jnp.einsum(
        "hqk,khd->qhd",
        weights.astype(jnp.bfloat16),
        values_grid,
        preferred_element_type=jnp.float32,
    )
    suffix_out = (summed / jnp.maximum(row_sum, 1.0).T[:, :, None]).astype(jnp.bfloat16)
    scaled_q = (rotated_q * scaling).astype(jnp.bfloat16)
    attended = prefix_attention(
        scaled_q.reshape(row_count, local_width),
        kv_rows,
        suffix_out.reshape(row_count, local_width),
        row_best[:, :, None],
        row_sum[:, :, None],
        alive.astype(jnp.float32)[:, None],
        head_count,
    )
    return (attended, suffix_cache.reshape(row_count, local_width))


def solution(mesh):
    placed = (
        P("req", "pre"),
        P("req", "pre"),
        P("req", "pre"),
        P("pre"),
        P("pre"),
        P("req", "pre"),
        P("req", "pre"),
        P("req", None),
        P("req"),
    )
    return jax.shard_map(
        per_device,
        mesh=mesh,
        in_specs=placed,
        out_specs=(P("req", "pre"), P("req", "pre")),
        check_vma=False,
    )
```

```python
import math

import jax
import jax.numpy as jnp
from jax import lax
from jax.experimental import pallas as pl
from jax.experimental.pallas import tpu as pltpu
from jax.sharding import PartitionSpec as P

HD = 128


epsilon = 1e-06
rope_base = 500000.0
floor_value = -1e30


def rotate(vectors, position):
    half_dim = vectors.shape[-1] // 2
    inverse = jnp.exp(
        -math.log(rope_base) * 2.0 * jnp.arange(half_dim, dtype=jnp.float32) / vectors.shape[-1]
    )
    angles = position.astype(jnp.float32)[:, None] * inverse[None, :]
    cosine = jnp.cos(angles)[:, None, :]
    sine_part = jnp.sin(angles)[:, None, :]
    first_half = vectors[..., :half_dim]
    second_half = vectors[..., half_dim:]
    return jnp.concatenate(
        [
            first_half * cosine - second_half * sine_part,
            second_half * cosine + first_half * sine_part,
        ],
        axis=-1,
    )


def positions(segment, prefix_len):
    row_index = jnp.arange(segment.shape[0], dtype=jnp.int32)
    first_row = jnp.sum((segment[None, :] < segment[:, None]).astype(jnp.int32), axis=1)
    return prefix_len + row_index - first_row


def flash_kernel(q_ref, k_ref, v_ref, oo_ref, om_ref, os_ref, alive_ref, out_ref, *, scaling):
    keys = k_ref[...].reshape(-1, HD)
    vals = v_ref[...].reshape(-1, HD)
    s = (
        lax.dot_general(
            q_ref[...],
            keys,
            (((1,), (1,)), ((), ())),
            preferred_element_type=jnp.float32,
        )
        * scaling
    )
    m = jnp.max(s, axis=1, keepdims=True)
    p = jnp.exp(s - m)
    prefix_sum = jnp.sum(p, axis=1, keepdims=True)
    prefix_acc = jnp.dot(p.astype(jnp.bfloat16), vals, preferred_element_type=jnp.float32)
    own_max = om_ref[...]
    best = jnp.maximum(m, own_max)
    prefix_weight = jnp.exp(m - best)
    own_weight = os_ref[...] * jnp.exp(own_max - best)
    numerator = prefix_acc * prefix_weight + own_weight * oo_ref[...].astype(jnp.float32)
    denominator = prefix_sum * prefix_weight + own_weight
    merged = numerator / denominator
    out_ref[...] = jnp.where(alive_ref[...] > 0.0, merged, 0.0).astype(out_ref.dtype)


def prefix_attention(queries2d, kv_rows, own_out2d, own_max, own_sum, alive_f, head_count, scaling):
    row_count = queries2d.shape[0]
    owners, _, shard_rows, _ = kv_rows.shape
    kernel = lambda *refs: flash_kernel(*refs, scaling=scaling)
    return pl.pallas_call(
        kernel,
        grid=(head_count,),
        in_specs=[
            pl.BlockSpec((row_count, HD), lambda h: (0, h)),
            pl.BlockSpec((owners, None, shard_rows, HD), lambda h: (0, 0, 0, h)),
            pl.BlockSpec((owners, None, shard_rows, HD), lambda h: (0, 1, 0, h)),
            pl.BlockSpec((row_count, HD), lambda h: (0, h)),
            pl.BlockSpec((None, row_count, 1), lambda h: (h, 0, 0)),
            pl.BlockSpec((None, row_count, 1), lambda h: (h, 0, 0)),
            pl.BlockSpec((row_count, 1), lambda h: (0, 0)),
        ],
        out_specs=pl.BlockSpec((row_count, HD), lambda h: (0, h)),
        out_shape=jax.ShapeDtypeStruct((row_count, head_count * HD), jnp.bfloat16),
        compiler_params=pltpu.CompilerParams(dimension_semantics=("arbitrary",)),
    )(queries2d, kv_rows, kv_rows, own_out2d, own_max, own_sum, alive_f)


def per_device(
    queries_raw,
    keys_raw,
    values,
    query_gain,
    key_gain,
    prefix_keys,
    prefix_values,
    segment_ids,
    live_rows,
):
    row_count, local_width = queries_raw.shape
    head_count = local_width // HD
    kv_block = jnp.stack([prefix_keys, prefix_values], axis=0)
    kv_rows = lax.all_gather(kv_block, "req", axis=0)
    query_f = queries_raw.astype(jnp.float32)
    key_f = keys_raw.astype(jnp.float32)
    square_q, square_k = lax.psum(
        (jnp.sum(query_f * query_f, axis=1), jnp.sum(key_f * key_f, axis=1)), "pre"
    )
    full_width = local_width * lax.axis_size("pre")
    normed_q = query_f * lax.rsqrt(square_q / full_width + epsilon)[:, None] * query_gain[None, :]
    normed_k = key_f * lax.rsqrt(square_k / full_width + epsilon)[:, None] * key_gain[None, :]
    shard_rows = prefix_keys.shape[0]
    prefix_len = shard_rows * lax.axis_size("req")
    segment = segment_ids[0]
    live_count = live_rows[0]
    position = positions(segment, prefix_len)
    queries_bf = rotate(normed_q.reshape(row_count, head_count, HD), position).astype(jnp.bfloat16)
    rotated_k = rotate(normed_k.reshape(row_count, head_count, HD), position).astype(jnp.bfloat16)
    row_index = jnp.arange(row_count, dtype=jnp.int32)
    alive = row_index < live_count
    suffix_cache = jnp.where(alive[:, None, None], rotated_k, jnp.zeros_like(rotated_k))
    values_grid = values.reshape(row_count, head_count, HD)
    scaling = 1.0 / math.sqrt(HD)
    scores = (
        jnp.einsum("qhd,khd->hqk", queries_bf, suffix_cache, preferred_element_type=jnp.float32)
        * scaling
    )
    allowed = (
        (segment[None, :] == segment[:, None])
        & (row_index[None, :] <= row_index[:, None])
        & alive[None, :]
    )
    row_best = jnp.max(jnp.where(allowed[None], scores, floor_value), axis=-1)
    weights = jnp.exp(jnp.where(allowed[None], scores - row_best[..., None], floor_value))
    row_sum = jnp.sum(weights, axis=-1)
    summed = jnp.einsum(
        "hqk,khd->qhd",
        weights.astype(jnp.bfloat16),
        values_grid,
        preferred_element_type=jnp.float32,
    )
    suffix_out = (summed / jnp.maximum(row_sum, 1.0).T[:, :, None]).astype(jnp.bfloat16)
    attended = prefix_attention(
        queries_bf.reshape(row_count, local_width),
        kv_rows,
        suffix_out.reshape(row_count, local_width),
        row_best[:, :, None],
        row_sum[:, :, None],
        alive.astype(jnp.float32)[:, None],
        head_count,
        scaling,
    )
    return (attended, suffix_cache.reshape(row_count, local_width))


def solution(mesh):
    placed = (
        P("req", "pre"),
        P("req", "pre"),
        P("req", "pre"),
        P("pre"),
        P("pre"),
        P("req", "pre"),
        P("req", "pre"),
        P("req", None),
        P("req"),
    )
    return jax.shard_map(
        per_device,
        mesh=mesh,
        in_specs=placed,
        out_specs=(P("req", "pre"), P("req", "pre")),
        check_vma=False,
    )
```

```python
import math

import jax
import jax.numpy as jnp
from jax import lax
from jax.experimental import pallas as pl
from jax.experimental.pallas import tpu as pltpu
from jax.sharding import PartitionSpec as P

HD = 128


epsilon = 1e-06
rope_base = 500000.0
floor_value = -1e30


def rotate(vectors, position):
    half_dim = vectors.shape[-1] // 2
    inverse = jnp.exp(
        -math.log(rope_base) * 2.0 * jnp.arange(half_dim, dtype=jnp.float32) / vectors.shape[-1]
    )
    angles = position.astype(jnp.float32)[:, None] * inverse[None, :]
    cosine = jnp.cos(angles)[:, None, :]
    sine_part = jnp.sin(angles)[:, None, :]
    first_half = vectors[..., :half_dim]
    second_half = vectors[..., half_dim:]
    return jnp.concatenate(
        [
            first_half * cosine - second_half * sine_part,
            second_half * cosine + first_half * sine_part,
        ],
        axis=-1,
    )


def positions(segment, prefix_len):
    row_index = jnp.arange(segment.shape[0], dtype=jnp.int32)
    first_row = jnp.sum((segment[None, :] < segment[:, None]).astype(jnp.int32), axis=1)
    return prefix_len + row_index - first_row


def flash_kernel(q_ref, k_ref, v_ref, oo_ref, om_ref, os_ref, alive_ref, out_ref, *, scaling):
    keys = k_ref[...].reshape(-1, HD)
    vals = v_ref[...].reshape(-1, HD)
    s = (
        lax.dot_general(
            q_ref[...],
            keys,
            (((1,), (1,)), ((), ())),
            preferred_element_type=jnp.float32,
        )
        * scaling
    )
    m = jnp.max(s, axis=1, keepdims=True)
    p = jnp.exp(s - m)
    prefix_sum = jnp.sum(p, axis=1, keepdims=True)
    prefix_acc = jnp.dot(p.astype(jnp.bfloat16), vals, preferred_element_type=jnp.float32)
    own_max = om_ref[...]
    best = jnp.maximum(m, own_max)
    prefix_weight = jnp.exp(m - best)
    own_weight = os_ref[...] * jnp.exp(own_max - best)
    numerator = prefix_acc * prefix_weight + own_weight * oo_ref[...].astype(jnp.float32)
    denominator = prefix_sum * prefix_weight + own_weight
    merged = numerator / denominator
    out_ref[...] = jnp.where(alive_ref[...] > 0.0, merged, 0.0).astype(out_ref.dtype)


def prefix_attention(queries2d, kv_rows, own_out2d, own_max, own_sum, alive_f, head_count, scaling):
    row_count = queries2d.shape[0]
    owners, _, shard_rows, _ = kv_rows.shape
    kernel = lambda *refs: flash_kernel(*refs, scaling=scaling)
    return pl.pallas_call(
        kernel,
        grid=(head_count,),
        in_specs=[
            pl.BlockSpec((row_count, HD), lambda h: (0, h)),
            pl.BlockSpec((owners, None, shard_rows, HD), lambda h: (0, 0, 0, h)),
            pl.BlockSpec((owners, None, shard_rows, HD), lambda h: (0, 1, 0, h)),
            pl.BlockSpec((row_count, HD), lambda h: (0, h)),
            pl.BlockSpec((None, row_count, 1), lambda h: (h, 0, 0)),
            pl.BlockSpec((None, row_count, 1), lambda h: (h, 0, 0)),
            pl.BlockSpec((row_count, 1), lambda h: (0, 0)),
        ],
        out_specs=pl.BlockSpec((row_count, HD), lambda h: (0, h)),
        out_shape=jax.ShapeDtypeStruct((row_count, head_count * HD), jnp.bfloat16),
        compiler_params=pltpu.CompilerParams(dimension_semantics=("arbitrary",)),
    )(queries2d, kv_rows, kv_rows, own_out2d, own_max, own_sum, alive_f)


def stack_kernel(k_hbm, v_hbm, out_hbm, sems):
    first = pltpu.make_async_copy(k_hbm, out_hbm.at[0], sems.at[0])
    second = pltpu.make_async_copy(v_hbm, out_hbm.at[1], sems.at[1])
    first.start()
    second.start()
    first.wait()
    second.wait()


def stack_pair(keys, vals):
    return pl.pallas_call(
        stack_kernel,
        in_specs=[pl.BlockSpec(memory_space=pl.ANY), pl.BlockSpec(memory_space=pl.ANY)],
        out_specs=pl.BlockSpec(memory_space=pl.ANY),
        out_shape=jax.ShapeDtypeStruct((2,) + keys.shape, keys.dtype),
        scratch_shapes=[pltpu.SemaphoreType.DMA((2,))],
    )(keys, vals)


def per_device(
    queries_raw,
    keys_raw,
    values,
    query_gain,
    key_gain,
    prefix_keys,
    prefix_values,
    segment_ids,
    live_rows,
):
    row_count, local_width = queries_raw.shape
    head_count = local_width // HD
    kv_block = stack_pair(prefix_keys, prefix_values)
    kv_rows = lax.all_gather(kv_block, "req", axis=0)
    query_f = queries_raw.astype(jnp.float32)
    key_f = keys_raw.astype(jnp.float32)
    square_q, square_k = lax.psum(
        (jnp.sum(query_f * query_f, axis=1), jnp.sum(key_f * key_f, axis=1)), "pre"
    )
    full_width = local_width * lax.axis_size("pre")
    normed_q = query_f * lax.rsqrt(square_q / full_width + epsilon)[:, None] * query_gain[None, :]
    normed_k = key_f * lax.rsqrt(square_k / full_width + epsilon)[:, None] * key_gain[None, :]
    shard_rows = prefix_keys.shape[0]
    prefix_len = shard_rows * lax.axis_size("req")
    segment = segment_ids[0]
    live_count = live_rows[0]
    position = positions(segment, prefix_len)
    queries_bf = rotate(normed_q.reshape(row_count, head_count, HD), position).astype(jnp.bfloat16)
    rotated_k = rotate(normed_k.reshape(row_count, head_count, HD), position).astype(jnp.bfloat16)
    row_index = jnp.arange(row_count, dtype=jnp.int32)
    alive = row_index < live_count
    suffix_cache = jnp.where(alive[:, None, None], rotated_k, jnp.zeros_like(rotated_k))
    values_grid = values.reshape(row_count, head_count, HD)
    scaling = 1.0 / math.sqrt(HD)
    scores = (
        jnp.einsum("qhd,khd->hqk", queries_bf, suffix_cache, preferred_element_type=jnp.float32)
        * scaling
    )
    allowed = (
        (segment[None, :] == segment[:, None])
        & (row_index[None, :] <= row_index[:, None])
        & alive[None, :]
    )
    row_best = jnp.max(jnp.where(allowed[None], scores, floor_value), axis=-1)
    weights = jnp.exp(jnp.where(allowed[None], scores - row_best[..., None], floor_value))
    row_sum = jnp.sum(weights, axis=-1)
    summed = jnp.einsum(
        "hqk,khd->qhd",
        weights.astype(jnp.bfloat16),
        values_grid,
        preferred_element_type=jnp.float32,
    )
    suffix_out = (summed / jnp.maximum(row_sum, 1.0).T[:, :, None]).astype(jnp.bfloat16)
    attended = prefix_attention(
        queries_bf.reshape(row_count, local_width),
        kv_rows,
        suffix_out.reshape(row_count, local_width),
        row_best[:, :, None],
        row_sum[:, :, None],
        alive.astype(jnp.float32)[:, None],
        head_count,
        scaling,
    )
    return (attended, suffix_cache.reshape(row_count, local_width))


def solution(mesh):
    placed = (
        P("req", "pre"),
        P("req", "pre"),
        P("req", "pre"),
        P("pre"),
        P("pre"),
        P("req", "pre"),
        P("req", "pre"),
        P("req", None),
        P("req"),
    )
    return jax.shard_map(
        per_device,
        mesh=mesh,
        in_specs=placed,
        out_specs=(P("req", "pre"), P("req", "pre")),
        check_vma=False,
    )
```

```python
import math

import jax
import jax.numpy as jnp
from jax import lax
from jax.experimental import pallas as pl
from jax.experimental.pallas import tpu as pltpu
from jax.sharding import PartitionSpec as P

HD = 128
LOG2_E = 1.4426950408889634


epsilon = 1e-06
rope_base = 500000.0
floor_value = -1e30


def rotate(vectors, position):
    half_dim = vectors.shape[-1] // 2
    inverse = jnp.exp(
        -math.log(rope_base) * 2.0 * jnp.arange(half_dim, dtype=jnp.float32) / vectors.shape[-1]
    )
    angles = position.astype(jnp.float32)[:, None] * inverse[None, :]
    cosine = jnp.cos(angles)[:, None, :]
    sine_part = jnp.sin(angles)[:, None, :]
    first_half = vectors[..., :half_dim]
    second_half = vectors[..., half_dim:]
    return jnp.concatenate(
        [
            first_half * cosine - second_half * sine_part,
            second_half * cosine + first_half * sine_part,
        ],
        axis=-1,
    )


def positions(segment, prefix_len):
    row_index = jnp.arange(segment.shape[0], dtype=jnp.int32)
    first_row = jnp.sum((segment[None, :] < segment[:, None]).astype(jnp.int32), axis=1)
    return prefix_len + row_index - first_row


def flash_kernel(q_ref, k_ref, v_ref, oo_ref, om_ref, os_ref, alive_ref, out_ref, *, scaling):
    keys = k_ref[...].reshape(-1, HD)
    vals = v_ref[...].reshape(-1, HD)
    s = lax.dot_general(
        q_ref[...],
        keys,
        (((1,), (1,)), ((), ())),
        preferred_element_type=jnp.float32,
    )
    top = jnp.max(s, axis=1, keepdims=True)
    p = jnp.exp2((s - top) * (scaling * LOG2_E))
    m = top * scaling
    prefix_sum = jnp.sum(p, axis=1, keepdims=True)
    prefix_acc = jnp.dot(p.astype(jnp.bfloat16), vals, preferred_element_type=jnp.float32)
    own_max = om_ref[...]
    best = jnp.maximum(m, own_max)
    prefix_weight = jnp.exp(m - best)
    own_weight = os_ref[...] * jnp.exp(own_max - best)
    numerator = prefix_acc * prefix_weight + own_weight * oo_ref[...].astype(jnp.float32)
    denominator = prefix_sum * prefix_weight + own_weight
    merged = numerator / denominator
    out_ref[...] = jnp.where(alive_ref[...] > 0.0, merged, 0.0).astype(out_ref.dtype)


def prefix_attention(queries2d, kv_rows, own_out2d, own_max, own_sum, alive_f, head_count, scaling):
    row_count = queries2d.shape[0]
    owners, _, shard_rows, _ = kv_rows.shape
    kernel = lambda *refs: flash_kernel(*refs, scaling=scaling)
    return pl.pallas_call(
        kernel,
        grid=(head_count,),
        in_specs=[
            pl.BlockSpec((row_count, HD), lambda h: (0, h)),
            pl.BlockSpec((owners, None, shard_rows, HD), lambda h: (0, 0, 0, h)),
            pl.BlockSpec((owners, None, shard_rows, HD), lambda h: (0, 1, 0, h)),
            pl.BlockSpec((row_count, HD), lambda h: (0, h)),
            pl.BlockSpec((None, row_count, 1), lambda h: (h, 0, 0)),
            pl.BlockSpec((None, row_count, 1), lambda h: (h, 0, 0)),
            pl.BlockSpec((row_count, 1), lambda h: (0, 0)),
        ],
        out_specs=pl.BlockSpec((row_count, HD), lambda h: (0, h)),
        out_shape=jax.ShapeDtypeStruct((row_count, head_count * HD), jnp.bfloat16),
        compiler_params=pltpu.CompilerParams(dimension_semantics=("arbitrary",)),
    )(queries2d, kv_rows, kv_rows, own_out2d, own_max, own_sum, alive_f)


def per_device(
    queries_raw,
    keys_raw,
    values,
    query_gain,
    key_gain,
    prefix_keys,
    prefix_values,
    segment_ids,
    live_rows,
):
    row_count, local_width = queries_raw.shape
    head_count = local_width // HD
    kv_block = jnp.stack([prefix_keys, prefix_values], axis=0)
    kv_rows = lax.all_gather(kv_block, "req", axis=0)
    query_f = queries_raw.astype(jnp.float32)
    key_f = keys_raw.astype(jnp.float32)
    square_q, square_k = lax.psum(
        (jnp.sum(query_f * query_f, axis=1), jnp.sum(key_f * key_f, axis=1)), "pre"
    )
    full_width = local_width * lax.axis_size("pre")
    normed_q = query_f * lax.rsqrt(square_q / full_width + epsilon)[:, None] * query_gain[None, :]
    normed_k = key_f * lax.rsqrt(square_k / full_width + epsilon)[:, None] * key_gain[None, :]
    shard_rows = prefix_keys.shape[0]
    prefix_len = shard_rows * lax.axis_size("req")
    segment = segment_ids[0]
    live_count = live_rows[0]
    position = positions(segment, prefix_len)
    queries_bf = rotate(normed_q.reshape(row_count, head_count, HD), position).astype(jnp.bfloat16)
    rotated_k = rotate(normed_k.reshape(row_count, head_count, HD), position).astype(jnp.bfloat16)
    row_index = jnp.arange(row_count, dtype=jnp.int32)
    alive = row_index < live_count
    suffix_cache = jnp.where(alive[:, None, None], rotated_k, jnp.zeros_like(rotated_k))
    values_grid = values.reshape(row_count, head_count, HD)
    scaling = 1.0 / math.sqrt(HD)
    scores = (
        jnp.einsum("qhd,khd->hqk", queries_bf, suffix_cache, preferred_element_type=jnp.float32)
        * scaling
    )
    allowed = (
        (segment[None, :] == segment[:, None])
        & (row_index[None, :] <= row_index[:, None])
        & alive[None, :]
    )
    row_best = jnp.max(jnp.where(allowed[None], scores, floor_value), axis=-1)
    weights = jnp.exp(jnp.where(allowed[None], scores - row_best[..., None], floor_value))
    row_sum = jnp.sum(weights, axis=-1)
    summed = jnp.einsum(
        "hqk,khd->qhd",
        weights.astype(jnp.bfloat16),
        values_grid,
        preferred_element_type=jnp.float32,
    )
    suffix_out = (summed / jnp.maximum(row_sum, 1.0).T[:, :, None]).astype(jnp.bfloat16)
    attended = prefix_attention(
        queries_bf.reshape(row_count, local_width),
        kv_rows,
        suffix_out.reshape(row_count, local_width),
        row_best[:, :, None],
        row_sum[:, :, None],
        alive.astype(jnp.float32)[:, None],
        head_count,
        scaling,
    )
    return (attended, suffix_cache.reshape(row_count, local_width))


def solution(mesh):
    placed = (
        P("req", "pre"),
        P("req", "pre"),
        P("req", "pre"),
        P("pre"),
        P("pre"),
        P("req", "pre"),
        P("req", "pre"),
        P("req", None),
        P("req"),
    )
    return jax.shard_map(
        per_device,
        mesh=mesh,
        in_specs=placed,
        out_specs=(P("req", "pre"), P("req", "pre")),
        check_vma=False,
    )
```

```python
import math

import jax
import jax.numpy as jnp
from jax import lax
from jax.experimental import pallas as pl
from jax.experimental.pallas import tpu as pltpu
from jax.sharding import PartitionSpec as P

HD = 128
LOG2_E = 1.4426950408889634


epsilon = 1e-06
rope_base = 500000.0
floor_value = -1e30


def rotate(vectors, position):
    half_dim = vectors.shape[-1] // 2
    inverse = jnp.exp(
        -math.log(rope_base) * 2.0 * jnp.arange(half_dim, dtype=jnp.float32) / vectors.shape[-1]
    )
    angles = position.astype(jnp.float32)[:, None] * inverse[None, :]
    cosine = jnp.cos(angles)[:, None, :]
    sine_part = jnp.sin(angles)[:, None, :]
    first_half = vectors[..., :half_dim]
    second_half = vectors[..., half_dim:]
    return jnp.concatenate(
        [
            first_half * cosine - second_half * sine_part,
            second_half * cosine + first_half * sine_part,
        ],
        axis=-1,
    )


def positions(segment, prefix_len):
    row_index = jnp.arange(segment.shape[0], dtype=jnp.int32)
    first_row = jnp.sum((segment[None, :] < segment[:, None]).astype(jnp.int32), axis=1)
    return prefix_len + row_index - first_row


def flash_kernel(q_ref, k_ref, v_ref, oo_ref, om_ref, os_ref, alive_ref, out_ref, *, scaling):
    keys = k_ref[...].reshape(-1, HD)
    vals = v_ref[...].reshape(-1, HD)
    s = lax.dot_general(
        q_ref[...],
        keys,
        (((1,), (1,)), ((), ())),
        preferred_element_type=jnp.float32,
    )
    top = jnp.max(s, axis=1, keepdims=True)
    p = jnp.exp2((s - top) * (scaling * LOG2_E))
    m = top * scaling
    prefix_sum = jnp.sum(p, axis=1, keepdims=True)
    prefix_acc = jnp.dot(p.astype(jnp.bfloat16), vals, preferred_element_type=jnp.float32)
    own_max = om_ref[...]
    best = jnp.maximum(m, own_max)
    prefix_weight = jnp.exp(m - best)
    own_weight = os_ref[...] * jnp.exp(own_max - best)
    numerator = prefix_acc * prefix_weight + own_weight * oo_ref[...].astype(jnp.float32)
    denominator = prefix_sum * prefix_weight + own_weight
    merged = numerator / denominator
    out_ref[...] = jnp.where(alive_ref[...] > 0.0, merged, 0.0).astype(out_ref.dtype)


def prefix_attention(queries2d, kv_rows, own_out2d, own_max, own_sum, alive_f, head_count, scaling):
    row_count = queries2d.shape[0]
    owners, _, shard_rows, _ = kv_rows.shape
    kernel = lambda *refs: flash_kernel(*refs, scaling=scaling)
    return pl.pallas_call(
        kernel,
        grid=(head_count,),
        in_specs=[
            pl.BlockSpec((row_count, HD), lambda h: (0, h)),
            pl.BlockSpec((owners, None, shard_rows, HD), lambda h: (0, 0, 0, h)),
            pl.BlockSpec((owners, None, shard_rows, HD), lambda h: (0, 1, 0, h)),
            pl.BlockSpec((row_count, HD), lambda h: (0, h)),
            pl.BlockSpec((None, row_count, 1), lambda h: (h, 0, 0)),
            pl.BlockSpec((None, row_count, 1), lambda h: (h, 0, 0)),
            pl.BlockSpec((row_count, 1), lambda h: (0, 0)),
        ],
        out_specs=pl.BlockSpec((row_count, HD), lambda h: (0, h)),
        out_shape=jax.ShapeDtypeStruct((row_count, head_count * HD), jnp.bfloat16),
        compiler_params=pltpu.CompilerParams(dimension_semantics=("arbitrary",)),
    )(queries2d, kv_rows, kv_rows, own_out2d, own_max, own_sum, alive_f)


def per_device(
    queries_raw,
    keys_raw,
    values,
    query_gain,
    key_gain,
    prefix_keys,
    prefix_values,
    segment_ids,
    live_rows,
):
    row_count, local_width = queries_raw.shape
    head_count = local_width // HD
    kv_block = lax.select(
        jnp.broadcast_to((jnp.arange(2) == 0)[:, None, None], (2,) + prefix_keys.shape),
        jnp.broadcast_to(prefix_keys[None], (2,) + prefix_keys.shape),
        jnp.broadcast_to(prefix_values[None], (2,) + prefix_keys.shape),
    )
    kv_rows = lax.all_gather(kv_block, "req", axis=0)
    query_f = queries_raw.astype(jnp.float32)
    key_f = keys_raw.astype(jnp.float32)
    square_q, square_k = lax.psum(
        (jnp.sum(query_f * query_f, axis=1), jnp.sum(key_f * key_f, axis=1)), "pre"
    )
    full_width = local_width * lax.axis_size("pre")
    normed_q = query_f * lax.rsqrt(square_q / full_width + epsilon)[:, None] * query_gain[None, :]
    normed_k = key_f * lax.rsqrt(square_k / full_width + epsilon)[:, None] * key_gain[None, :]
    shard_rows = prefix_keys.shape[0]
    prefix_len = shard_rows * lax.axis_size("req")
    segment = segment_ids[0]
    live_count = live_rows[0]
    position = positions(segment, prefix_len)
    queries_bf = rotate(normed_q.reshape(row_count, head_count, HD), position).astype(jnp.bfloat16)
    rotated_k = rotate(normed_k.reshape(row_count, head_count, HD), position).astype(jnp.bfloat16)
    row_index = jnp.arange(row_count, dtype=jnp.int32)
    alive = row_index < live_count
    suffix_cache = jnp.where(alive[:, None, None], rotated_k, jnp.zeros_like(rotated_k))
    values_grid = values.reshape(row_count, head_count, HD)
    scaling = 1.0 / math.sqrt(HD)
    scores = (
        jnp.einsum("qhd,khd->hqk", queries_bf, suffix_cache, preferred_element_type=jnp.float32)
        * scaling
    )
    allowed = (
        (segment[None, :] == segment[:, None])
        & (row_index[None, :] <= row_index[:, None])
        & alive[None, :]
    )
    row_best = jnp.max(jnp.where(allowed[None], scores, floor_value), axis=-1)
    weights = jnp.exp(jnp.where(allowed[None], scores - row_best[..., None], floor_value))
    row_sum = jnp.sum(weights, axis=-1)
    summed = jnp.einsum(
        "hqk,khd->qhd",
        weights.astype(jnp.bfloat16),
        values_grid,
        preferred_element_type=jnp.float32,
    )
    suffix_out = (summed / jnp.maximum(row_sum, 1.0).T[:, :, None]).astype(jnp.bfloat16)
    attended = prefix_attention(
        queries_bf.reshape(row_count, local_width),
        kv_rows,
        suffix_out.reshape(row_count, local_width),
        row_best[:, :, None],
        row_sum[:, :, None],
        alive.astype(jnp.float32)[:, None],
        head_count,
        scaling,
    )
    return (attended, suffix_cache.reshape(row_count, local_width))


def solution(mesh):
    placed = (
        P("req", "pre"),
        P("req", "pre"),
        P("req", "pre"),
        P("pre"),
        P("pre"),
        P("req", "pre"),
        P("req", "pre"),
        P("req", None),
        P("req"),
    )
    return jax.shard_map(
        per_device,
        mesh=mesh,
        in_specs=placed,
        out_specs=(P("req", "pre"), P("req", "pre")),
        check_vma=False,
    )
```

```python
import math

import jax
import jax.numpy as jnp
from jax import lax
from jax.experimental import pallas as pl
from jax.experimental.pallas import tpu as pltpu
from jax.sharding import PartitionSpec as P

HD = 128
LOG2_E = 1.4426950408889634


epsilon = 1e-06
rope_base = 500000.0
floor_value = -1e30


def rotate(vectors, position):
    half_dim = vectors.shape[-1] // 2
    inverse = jnp.exp(
        -math.log(rope_base) * 2.0 * jnp.arange(half_dim, dtype=jnp.float32) / vectors.shape[-1]
    )
    angles = position.astype(jnp.float32)[:, None] * inverse[None, :]
    cosine = jnp.cos(angles)[:, None, :]
    sine_part = jnp.sin(angles)[:, None, :]
    first_half = vectors[..., :half_dim]
    second_half = vectors[..., half_dim:]
    return jnp.concatenate(
        [
            first_half * cosine - second_half * sine_part,
            second_half * cosine + first_half * sine_part,
        ],
        axis=-1,
    )


def positions(segment, prefix_len):
    row_index = jnp.arange(segment.shape[0], dtype=jnp.int32)
    first_row = jnp.sum((segment[None, :] < segment[:, None]).astype(jnp.int32), axis=1)
    return prefix_len + row_index - first_row


def flash_kernel(qt_ref, k_ref, v_ref, oo_ref, om_ref, os_ref, alive_ref, out_ref, *, scaling):
    keys = k_ref[...].reshape(-1, HD)
    vals = v_ref[...].reshape(-1, HD)
    scores_t = jnp.dot(keys, qt_ref[...], preferred_element_type=jnp.float32)
    top = jnp.max(scores_t, axis=0, keepdims=True)
    probs_t = jnp.exp2((scores_t - top) * (scaling * LOG2_E))
    prefix_sum = jnp.sum(probs_t, axis=0, keepdims=True)
    prefix_acc = lax.dot_general(
        vals,
        probs_t.astype(jnp.bfloat16),
        (((0,), (0,)), ((), ())),
        preferred_element_type=jnp.float32,
    )
    m = top * scaling
    own_max = om_ref[...]
    best = jnp.maximum(m, own_max)
    prefix_weight = jnp.exp(m - best)
    own_weight = os_ref[...] * jnp.exp(own_max - best)
    numerator = prefix_acc * prefix_weight + own_weight * oo_ref[...].astype(jnp.float32)
    denominator = prefix_sum * prefix_weight + own_weight
    merged = jnp.where(alive_ref[...] > 0.0, numerator / denominator, 0.0)
    out_ref[...] = merged.T.astype(out_ref.dtype)


def prefix_attention(queries_t, kv_rows, own_out_t, own_max, own_sum, alive_f, head_count, scaling):
    row_count = queries_t.shape[1]
    owners, _, shard_rows, _ = kv_rows.shape
    kernel = lambda *refs: flash_kernel(*refs, scaling=scaling)
    return pl.pallas_call(
        kernel,
        grid=(head_count,),
        in_specs=[
            pl.BlockSpec((HD, row_count), lambda h: (h, 0)),
            pl.BlockSpec((owners, None, shard_rows, HD), lambda h: (0, 0, 0, h)),
            pl.BlockSpec((owners, None, shard_rows, HD), lambda h: (0, 1, 0, h)),
            pl.BlockSpec((HD, row_count), lambda h: (h, 0)),
            pl.BlockSpec((None, 1, row_count), lambda h: (h, 0, 0)),
            pl.BlockSpec((None, 1, row_count), lambda h: (h, 0, 0)),
            pl.BlockSpec((1, row_count), lambda h: (0, 0)),
        ],
        out_specs=pl.BlockSpec((row_count, HD), lambda h: (0, h)),
        out_shape=jax.ShapeDtypeStruct((row_count, head_count * HD), jnp.bfloat16),
        compiler_params=pltpu.CompilerParams(dimension_semantics=("arbitrary",)),
    )(queries_t, kv_rows, kv_rows, own_out_t, own_max, own_sum, alive_f)


def per_device(
    queries_raw,
    keys_raw,
    values,
    query_gain,
    key_gain,
    prefix_keys,
    prefix_values,
    segment_ids,
    live_rows,
):
    row_count, local_width = queries_raw.shape
    head_count = local_width // HD
    kv_block = jnp.stack([prefix_keys, prefix_values], axis=0)
    kv_rows = lax.all_gather(kv_block, "req", axis=0)
    query_f = queries_raw.astype(jnp.float32)
    key_f = keys_raw.astype(jnp.float32)
    square_q, square_k = lax.psum(
        (jnp.sum(query_f * query_f, axis=1), jnp.sum(key_f * key_f, axis=1)), "pre"
    )
    full_width = local_width * lax.axis_size("pre")
    normed_q = query_f * lax.rsqrt(square_q / full_width + epsilon)[:, None] * query_gain[None, :]
    normed_k = key_f * lax.rsqrt(square_k / full_width + epsilon)[:, None] * key_gain[None, :]
    shard_rows = prefix_keys.shape[0]
    prefix_len = shard_rows * lax.axis_size("req")
    segment = segment_ids[0]
    live_count = live_rows[0]
    position = positions(segment, prefix_len)
    queries_bf = rotate(normed_q.reshape(row_count, head_count, HD), position).astype(jnp.bfloat16)
    rotated_k = rotate(normed_k.reshape(row_count, head_count, HD), position).astype(jnp.bfloat16)
    row_index = jnp.arange(row_count, dtype=jnp.int32)
    alive = row_index < live_count
    suffix_cache = jnp.where(alive[:, None, None], rotated_k, jnp.zeros_like(rotated_k))
    values_grid = values.reshape(row_count, head_count, HD)
    scaling = 1.0 / math.sqrt(HD)
    scores = (
        jnp.einsum("qhd,khd->hqk", queries_bf, suffix_cache, preferred_element_type=jnp.float32)
        * scaling
    )
    allowed = (
        (segment[None, :] == segment[:, None])
        & (row_index[None, :] <= row_index[:, None])
        & alive[None, :]
    )
    row_best = jnp.max(jnp.where(allowed[None], scores, floor_value), axis=-1)
    weights = jnp.exp(jnp.where(allowed[None], scores - row_best[..., None], floor_value))
    row_sum = jnp.sum(weights, axis=-1)
    summed = jnp.einsum(
        "hqk,khd->hdq",
        weights.astype(jnp.bfloat16),
        values_grid,
        preferred_element_type=jnp.float32,
    )
    suffix_out_t = (summed / jnp.maximum(row_sum, 1.0)[:, None, :]).astype(jnp.bfloat16)
    queries_t = jnp.transpose(queries_bf, (1, 2, 0)).reshape(local_width, row_count)
    attended = prefix_attention(
        queries_t,
        kv_rows,
        suffix_out_t.reshape(local_width, row_count),
        row_best[:, None, :],
        row_sum[:, None, :],
        alive.astype(jnp.float32)[None, :],
        head_count,
        scaling,
    )
    return (attended, suffix_cache.reshape(row_count, local_width))


def solution(mesh):
    placed = (
        P("req", "pre"),
        P("req", "pre"),
        P("req", "pre"),
        P("pre"),
        P("pre"),
        P("req", "pre"),
        P("req", "pre"),
        P("req", None),
        P("req"),
    )
    return jax.shard_map(
        per_device,
        mesh=mesh,
        in_specs=placed,
        out_specs=(P("req", "pre"), P("req", "pre")),
        check_vma=False,
    )
```
